32 devices in a mesh: groups: 2 (over x), freq: 16 (over z, y, core).
Axes of the slice: x: 2, y: 2, z: 4, core: 2. Of those that a mesh axis runs over, the one named last changes fastest.
Arguments:
- volts: bfloat16 [256, 68608], P(('groups', 'freq')), parts along dimension 0, may hold values from -6 to 6
- filter_taps: float32 [4, 1024], replicated, may hold values from -3 to 3
- kernel: float32 [63], replicated, may hold values from -0.5 to 0.5
Outputs:
- smoothed: bfloat16 [512, 256, 128], P(None, ('groups', 'freq')), parts along dimension 1
The draws below stay inside these ranges and needn't reach their ends.
There are 2 independent parts, one for each index of `groups`. The reference program is written for one: setup_inputs(seed, part) draws one part's arguments, and reference() takes and returns one part's arrays. A program takes and returns all parts, laid end to end along the dimension named above; an argument that names none is the same for every part. Nothing has to cross between parts.
All inputs are finite; a program needn't handle non-finite values.
Results may differ from the reference program's by a relative error of at most 0.011.
Values may be sent and summed in bfloat16 or wider, within the bound.
A program may use at most 128 MiB of HBM per device.

```python
import jax
import jax.numpy as jnp
from jax import lax

CH = 512
FRAME = 1024
TAPS = 4
KERNEL = 63
SPEC = 64
INPUTS = 128
SAMPLES = 68608


def levels(key, extent, split, least, top_value):
    level, own = 1.0, jax.random.fold_in(key, 6)
    for position, shards_of in split:
        draws = jnp.exp(jax.random.uniform(jax.random.fold_in(own, position), (shards_of,), jnp.float32, least / len(split), top_value / len(split)))
        level = level * jnp.repeat(draws, extent[position] // shards_of).reshape([-1 if axis == position else 1 for axis in range(len(extent))])
    return level


def scatter_about(rng, dims, spread, bound, shards=(), kind=jnp.bfloat16):
    loudness = levels(rng, dims, shards, -0.22, 0.18) if shards else 1.0
    drawn = jax.random.normal(rng, dims, jnp.float32) * spread * loudness
    return jnp.minimum(jnp.maximum(drawn, -bound), bound).astype(kind)


def setup_inputs(seed: int = 0, part: int = 0) -> dict:
    seeds = jax.random.split(jax.random.key(seed), 4)
    part_keys = jax.random.split(jax.random.fold_in(seeds[3], part), 4)
    volts = scatter_about(part_keys[0], (INPUTS, SAMPLES), 1.0, 6.0, ((0, 16),))
    filter_taps = scatter_about(seeds[1], (TAPS, FRAME), 0.5, 3.0, (), jnp.float32)
    kernel = scatter_about(seeds[2], (KERNEL,), 0.125, 0.5, (), jnp.float32)
    return dict(volts=volts, filter_taps=filter_taps, kernel=kernel)


def make_table(frame, channels):
    rows = jnp.arange(frame, dtype=jnp.int32)
    cols = jnp.arange(channels, dtype=jnp.int32)
    phase = (2 * rows[:, None] + 1 + channels) * (2 * cols[None, :] + 1) % (8 * channels)
    angle = phase.astype(jnp.float32) * (jnp.pi / (4.0 * channels))
    return (jnp.cos(angle) * (1.0 / jnp.sqrt(jnp.float32(channels)))).astype(jnp.bfloat16)

def reference(volts, filter_taps, kernel):
    blocks = volts.reshape(INPUTS, SPEC + TAPS - 1, FRAME).astype(jnp.float32)
    filtered = jnp.zeros((INPUTS, SPEC, FRAME), jnp.float32)
    for tap in range(TAPS):
        filtered = filtered + filter_taps[tap][None, None, :] * blocks[:, tap:tap + SPEC, :]
    filtered = filtered.astype(jnp.bfloat16)
    table = make_table(FRAME, CH)
    chan = jnp.dot(filtered.reshape(INPUTS * SPEC, FRAME), table, preferred_element_type=jnp.float32)
    chan = chan.astype(jnp.bfloat16).reshape(INPUTS, SPEC, CH).astype(jnp.float32)
    weights = kernel.astype(jnp.bfloat16).astype(jnp.float32)
    half = (KERNEL - 1) // 2
    row_block = min(64, INPUTS)

    def one_block(start):
        rows = lax.dynamic_slice_in_dim(chan, start, row_block, 0)
        vis = jnp.einsum('isc,jsc->cij', rows, chan) * (1.0 / jnp.sqrt(jnp.float32(SPEC)))
        vis = lax.optimization_barrier(vis.astype(jnp.bfloat16)).astype(jnp.float32)
        padded = jnp.pad(vis, ((half, half), (0, 0), (0, 0)))
        total = jnp.zeros_like(vis)
        for step in range(KERNEL):
            total = total + weights[step] * padded[step:step + CH]
        return total.astype(jnp.bfloat16)
    starts = jnp.arange(0, INPUTS, row_block, dtype=jnp.int32)
    result = lax.map(one_block, starts)
    return result.transpose(1, 0, 2, 3).reshape(CH, INPUTS, INPUTS)
```

```python
import functools

import jax
import jax.numpy as jnp
import ml_dtypes
import numpy as np
from jax import lax
from jax.experimental import pallas as pl
from jax.experimental.pallas import tpu as pltpu
from jax.sharding import PartitionSpec as P

NT = (((1,), (1,)), ((), ()))


def make_table(frame, channels, devices):
    order = np.arange(channels).reshape(devices, channels // devices // 2, 2)
    order = order.transpose(2, 0, 1).reshape(-1)
    rows = np.arange(frame)
    phase = (2 * rows[None, :] + 1 + channels) * (2 * order[:, None] + 1) % (8 * channels)
    angle = phase.astype(np.float32) * np.float32(np.pi / (4.0 * channels))
    scale = np.float32(1.0) / np.sqrt(np.float32(channels))
    return (np.cos(angle) * scale).astype(ml_dtypes.bfloat16)


def correlate(
    n, chunks, volts_hbm, taps_hbm, table_hbm, vis_out, packed_out,
    volts, taps, table,
    frames, framesb, product, chan_f, chan_send, chan_recv, chan_half,
    vis_send, half_send, cross_send,
    sent, got, fetched, stored,
):
    groups = lax.axis_index("groups")
    me = lax.axis_index("freq")
    m = n // 2
    side = lax.div(me, m)
    place = lax.rem(me, m)
    ntaps, frame = taps.shape
    channels = table.shape[0]
    inp, samples = volts.shape
    spectra = samples // frame - ntaps + 1
    pairs = channels // n // 2
    step = pairs // chunks
    inputs = n * inp
    half = channels // 2

    barrier = pltpu.get_barrier_semaphore()

    def greet(p, _):
        pl.semaphore_signal(
            barrier, inc=1, device_id=(groups, lax.rem(me + p, n)),
            device_id_type=pl.DeviceIdType.MESH,
        )
        return 0

    lax.fori_loop(1, n, greet, 0)

    fetch = [
        pltpu.make_async_copy(volts_hbm, volts, fetched.at[0]),
        pltpu.make_async_copy(taps_hbm, taps, fetched.at[1]),
        pltpu.make_async_copy(table_hbm, table, fetched.at[2]),
    ]
    for copy in fetch:
        copy.start()
    fetch[0].wait()
    fetch[1].wait()

    def filter_lanes(mb, _):
        base = pl.multiple_of(mb * 128, 128)
        weights = [jnp.broadcast_to(taps[t : t + 1, pl.ds(base, 128)], (inp, 128)) for t in range(ntaps)]

        def block(s):
            at = pl.multiple_of(s * frame + base, 128)
            return volts[:, pl.ds(at, 128)].astype(jnp.float32)

        held = [block(s) for s in range(ntaps - 1)]
        for s in range(spectra):
            held.append(block(s + ntaps - 1))
            total = weights[0] * held[0]
            for t in range(1, ntaps):
                total = total + weights[t] * held[t]
            frames.at[mb][pl.ds(s * inp, inp), :] = total
            held = held[1:]
        return 0

    lax.fori_loop(0, frame // 128, filter_lanes, 0)
    for mb in range(frame // 128):
        for i in range(inp):
            framesb[i * spectra : (i + 1) * spectra, mb * 128 : (mb + 1) * 128] = (
                frames.at[mb][pl.ds(i, spectra, stride=inp), :].astype(jnp.bfloat16)
            )

    fetch[2].wait()
    product[...] = lax.dot_general(table[...], framesb[...], NT, preferred_element_type=jnp.float32)
    low = lax.broadcasted_iota(jnp.int32, (half, 128), 1) < spectra
    for p in range(inp // 2):
        even = product[:half, 128 * p : 128 * (p + 1)]
        odd = product[half:, 128 * p : 128 * (p + 1)]
        chan_f[pl.ds(2 * p, half, stride=inp), :] = jnp.where(low, even, pltpu.roll(odd, spectra, 1))
        chan_f[pl.ds(2 * p + 1, half, stride=inp), :] = jnp.where(low, pltpu.roll(even, spectra, 1), odd)
    chan_send[...] = chan_f[...].reshape(n, pairs, inp, 128).astype(jnp.bfloat16)

    def remote(src, dst, send_sem, recv_sem, peer):
        return pltpu.make_async_remote_copy(
            src_ref=src, dst_ref=dst, send_sem=send_sem, recv_sem=recv_sem,
            device_id=(groups, peer), device_id_type=pl.DeviceIdType.MESH,
        )

    def arrived(whole, kind, c):
        remote(whole, whole, sent.at[kind], got.at[kind, c], (1 - side) * m + place).wait_recv()

    def departed(whole, kind):
        remote(whole, whole, sent.at[kind], got.at[kind, 0], (1 - side) * m + place).wait_send()

    def full_chan(c, peer, source):
        at = pl.ds(c * step, step)
        owner = 2 * lax.rem(peer, m) + lax.div(peer, m)
        return remote(
            chan_send.at[owner, at], chan_recv.at[source, at],
            sent.at[0], got.at[0, c], peer,
        )

    def half_chan(c, spot, source):
        at = pl.ds(c * step, step)
        return remote(
            chan_send.at[2 * spot + 1 - side, at], chan_half.at[source, at],
            sent.at[1], got.at[1, c], side * m + spot,
        )

    def full_vis(c, spot, source):
        at = pl.ds(c * step, step)
        return remote(
            vis_send.at[spot, at], vis_out.at[source, at],
            sent.at[2], got.at[2, c], side * m + spot,
        )

    def half_vis(c, spot, source):
        at = pl.ds(c * step, step)
        return remote(
            half_send.at[spot, at], packed_out.at[side, source, at],
            sent.at[3], got.at[3, c], side * m + spot,
        )

    def cross_vis(c, spot, source, column_side):
        at = pl.ds(c * step, step)
        return remote(
            cross_send.at[spot, at], packed_out.at[column_side, source, at],
            sent.at[4], got.at[4, c], (1 - side) * m + spot,
        )

    def loop(first, act):
        def body(p, _):
            act(lax.rem(place + p, m))
            return 0

        lax.fori_loop(first, m, body, 0)

    pl.semaphore_wait(barrier, n - 1)
    for c in range(chunks):

        def mixed(spot):
            full_chan(c, (1 - side) * m + spot, me).start()

            @pl.when(spot != place)
            def _():
                full_chan(c, side * m + spot, me).start()
                half_chan(c, spot, place).start()

        loop(0, mixed)
    chan_recv[me] = chan_send[2 * place + side]
    chan_half[place] = chan_send[2 * place + 1 - side]

    scale = 1.0 / (spectra**0.5)
    ours = inputs // 2
    first = lax.broadcasted_iota(jnp.int32, (ours, 128), 1) < spectra

    def rows_of(value):
        return value.astype(jnp.float32).reshape(-1, 128)

    def product_of(left, right):
        return lax.dot_general(left, right, NT, preferred_element_type=jnp.float32) * scale

    def parities(value):
        return [
            jnp.where(first, value, 0.0).astype(jnp.bfloat16),
            jnp.where(first, 0.0, value).astype(jnp.bfloat16),
        ]

    for c in range(chunks):
        at = pl.ds(c * step, step)
        arrived(chan_recv.at[pl.ds(0, n - 1), at], 0, c)
        arrived(chan_half.at[pl.ds(0, m - 1), at], 1, c)

        def gram(k, _):
            every = rows_of(chan_recv[:, k]).astype(jnp.bfloat16)
            own = parities(rows_of(chan_recv[pl.ds(side * m, m), k]))
            other = rows_of(chan_recv[pl.ds((1 - side) * m, m), k]).astype(jnp.bfloat16)
            cross = product_of(other, jnp.concatenate(own, axis=0))
            cross_send[:, k] = cross.reshape(m, inp, inputs).astype(jnp.bfloat16)
            for parity in range(2):
                full = product_of(own[parity], every)
                vis_send[:, k, parity] = full.reshape(m, inp, inputs).astype(jnp.bfloat16)
            mine = rows_of(chan_half[:, k])
            within = product_of(mine.astype(jnp.bfloat16), jnp.concatenate(parities(mine), axis=0))
            half_send[:, k] = within.reshape(m, inp, inputs).astype(jnp.bfloat16)
            return 0

        lax.fori_loop(c * step, (c + 1) * step, gram, 0)

        def mixed_vis(spot):
            cross_vis(c, spot, place, side).start()

            @pl.when(spot != place)
            def _():
                full_vis(c, spot, place).start()
                half_vis(c, spot, place).start()

        loop(0, mixed_vis)
    kept = [
        pltpu.make_async_copy(vis_send.at[place], vis_out.at[place], stored.at[0]),
        pltpu.make_async_copy(half_send.at[place], packed_out.at[side, place], stored.at[1]),
    ]
    for copy in kept:
        copy.start()
    for c in range(chunks):
        at = pl.ds(c * step, step)
        arrived(vis_out.at[pl.ds(0, m - 1), at], 2, c)
        arrived(packed_out.at[side, pl.ds(0, m - 1), at], 3, c)
        arrived(packed_out.at[1 - side, pl.ds(0, m), at], 4, c)
    departed(chan_send.at[pl.ds(0, n - 1)], 0)
    departed(chan_send.at[pl.ds(0, m - 1)], 1)
    departed(vis_send.at[pl.ds(0, m - 1)], 2)
    departed(half_send.at[pl.ds(0, m - 1)], 3)
    departed(cross_send.at[pl.ds(0, m)], 4)
    for copy in kept:
        copy.wait()


def smooth_all(vis_in, packed, kernel, out_hbm, vis, rows_f, planes, window, out, stored):
    side = lax.div(lax.axis_index("freq"), vis_in.shape[0])
    m, pairs, _, inp, inputs = vis_in.shape
    channels = out.shape[0]
    ours = inputs // 2
    count = kernel.shape[1]
    reach = (count - 1) // 2
    window[...] = jnp.zeros_like(window)
    window[0:1, 0:count] = kernel[...].astype(jnp.bfloat16).astype(jnp.float32)
    spread = jnp.broadcast_to(window[0:1, :], (128, 256))
    band = pltpu.roll(spread, 64 - reach, 1, stride=1, stride_axis=0).astype(jnp.bfloat16)
    lower = lax.broadcasted_iota(jnp.int32, (pairs, inp, inputs), 2) < ours

    def unpack(spot, _):
        left = packed[0, spot].astype(jnp.float32)
        right = packed[1, spot].astype(jnp.float32)
        even = jnp.where(lower, left, pltpu.roll(right, ours, 2))
        odd = jnp.where(lower, pltpu.roll(left, ours, 2), right)
        vis[spot, 1 - side, :, 0] = even.astype(jnp.bfloat16)
        vis[spot, 1 - side, :, 1] = odd.astype(jnp.bfloat16)
        vis[spot, side] = vis_in[spot]
        return 0

    lax.fori_loop(0, m, unpack, 0)

    planes[0:64, :] = jnp.zeros((64, inp * 128), jnp.bfloat16)
    planes[64 + channels :, :] = jnp.zeros((64, inp * 128), jnp.bfloat16)

    def smooth(j, _):
        lanes = pl.ds(pl.multiple_of(j * 128, 128), 128)
        rows_f[...] = vis[:, :, :, :, :, lanes].astype(jnp.float32).reshape(channels * inp, 128)
        for i in range(inp):
            planes[64 : 64 + channels, i * 128 : (i + 1) * 128] = (
                rows_f[pl.ds(i, channels, stride=inp), :].astype(jnp.bfloat16)
            )
        for r in range(channels // 128):
            done = jnp.dot(band, planes[r * 128 : r * 128 + 256, :], preferred_element_type=jnp.float32)
            for i in range(inp):
                rows_f[pl.ds(r * 128 * inp + i, 128, stride=inp), :] = done[:, i * 128 : (i + 1) * 128]
            rows = rows_f[r * 128 * inp : (r + 1) * 128 * inp, :]
            out[r * 128 : (r + 1) * 128, :, lanes] = rows.reshape(128, inp, 128).astype(jnp.bfloat16)
            pltpu.make_async_copy(
                out.at[r * 128 : (r + 1) * 128, :, lanes],
                out_hbm.at[r * 128 : (r + 1) * 128, :, lanes],
                stored.at[0],
            ).start()
        return 0

    lax.fori_loop(0, inputs // 128, smooth, 0)
    pltpu.make_async_copy(out, out_hbm, stored.at[0]).wait()


def shards(volts, filter_taps, kernel):
    inp, samples = volts.shape
    ntaps, frame = filter_taps.shape
    channels = frame // 2
    spectra = samples // frame - ntaps + 1
    n = lax.axis_size("freq")
    ch_dev = channels // n
    pairs = ch_dev // 2
    inputs = n * inp
    chunks = min(2, pairs)
    table = jnp.asarray(make_table(frame, channels, n))
    vmem = pl.BlockSpec(memory_space=pltpu.VMEM)
    hbm = pl.BlockSpec(memory_space=pl.ANY)
    far = pl.BlockSpec(memory_space=pltpu.HBM)
    bf16, f32 = jnp.bfloat16, jnp.float32
    half = n // 2
    vis, packed = pl.pallas_call(
        functools.partial(correlate, n, chunks),
        out_shape=[
            jax.ShapeDtypeStruct((half, pairs, 2, inp, inputs), bf16),
            jax.ShapeDtypeStruct((2, half, pairs, inp, inputs), bf16),
        ],
        in_specs=[far, far, far],
        out_specs=[hbm, hbm],
        scratch_shapes=[
            pltpu.VMEM(volts.shape, bf16),
            pltpu.VMEM(filter_taps.shape, f32),
            pltpu.VMEM(table.shape, bf16),
            pltpu.VMEM((frame // 128, inp * spectra, 128), f32),
            pltpu.VMEM((inp * spectra, frame), bf16),
            pltpu.VMEM((channels, inp * spectra), f32),
            pltpu.VMEM((channels // 2 * inp, 128), f32),
            pltpu.VMEM((n, pairs, inp, 128), bf16),
            pltpu.VMEM((n, pairs, inp, 128), bf16),
            pltpu.VMEM((n // 2, pairs, inp, 128), bf16),
            pltpu.VMEM((n // 2, pairs, 2, inp, inputs), bf16),
            pltpu.VMEM((n // 2, pairs, inp, inputs), bf16),
            pltpu.VMEM((n // 2, pairs, inp, inputs), bf16),
            pltpu.SemaphoreType.DMA((5,)),
            pltpu.SemaphoreType.DMA((5, chunks)),
            pltpu.SemaphoreType.DMA((3,)),
            pltpu.SemaphoreType.DMA((2,)),
        ],
        compiler_params=pltpu.CompilerParams(
            collective_id=0, has_side_effects=True, vmem_limit_bytes=52 << 20
        ),
        name="correlate",
    )(volts, filter_taps, table)
    return pl.pallas_call(
        smooth_all,
        out_shape=jax.ShapeDtypeStruct((channels, inp, inputs), bf16),
        in_specs=[vmem, vmem, vmem],
        out_specs=hbm,
        scratch_shapes=[
            pltpu.VMEM((half, 2, pairs, 2, inp, inputs), bf16),
            pltpu.VMEM((channels * inp, 128), f32),
            pltpu.VMEM((channels + 128, inp * 128), bf16),
            pltpu.VMEM((8, 256), f32),
            pltpu.VMEM((channels, inp, inputs), bf16),
            pltpu.SemaphoreType.DMA((1,)),
        ],
        compiler_params=pltpu.CompilerParams(vmem_limit_bytes=24 << 20),
        name="smooth",
    )(vis, packed, kernel.reshape(1, -1))


def solution(mesh):
    return jax.shard_map(
        shards,
        mesh=mesh,
        in_specs=(P(("groups", "freq"), None), P(), P()),
        out_specs=P(None, ("groups", "freq"), None),
        check_vma=False,
    )
```

```python
import functools

import jax
import jax.numpy as jnp
import ml_dtypes
import numpy as np
from jax import lax
from jax.experimental import pallas as pl
from jax.experimental.pallas import tpu as pltpu
from jax.sharding import PartitionSpec as P

CHUNKS = 8
PARTS = 2
NT = (((1,), (1,)), ((), ()))


def make_table(frame, channels, owners, parts):
    order = np.arange(channels).reshape(owners, parts, channels // owners // parts // 2, 2)
    order = order.transpose(1, 3, 0, 2).reshape(-1)
    rows = np.arange(frame)
    phase = (2 * rows[None, :] + 1 + channels) * (2 * order[:, None] + 1) % (8 * channels)
    angle = phase.astype(np.float32) * np.float32(np.pi / (4.0 * channels))
    scale = np.float32(1.0) / np.sqrt(np.float32(channels))
    return (np.cos(angle) * scale).astype(ml_dtypes.bfloat16)


def correlate(
    n, chunks, parts, volts_hbm, taps_hbm, table_hbm, vis_out, packed_out,
    volts, taps, table,
    frames, framesb, product, chan_f, chan_send, chan_recv, chan_half,
    vis_send, half_send, cross_send,
    sent, got, fetched, stored,
):
    groups = lax.axis_index("groups")
    me = lax.axis_index("freq")
    m = n // 2
    h = m // 2
    side = lax.div(me, m)
    place = lax.rem(me, m)
    spot_of = lax.rem(place, h)
    inner = lax.div(place, h) != side
    ntaps, frame = taps.shape
    channels = table.shape[0]
    inp, samples = volts.shape
    spectra = samples // frame - ntaps + 1
    pairs = channels // m // 2
    step = pairs // chunks
    inputs = n * inp
    half = channels // 2 // parts

    barrier = pltpu.get_barrier_semaphore()

    def greet(p, _):
        pl.semaphore_signal(
            barrier, inc=1, device_id=(groups, lax.rem(me + p, n)),
            device_id_type=pl.DeviceIdType.MESH,
        )
        return 0

    lax.fori_loop(1, n, greet, 0)

    fetch = [
        pltpu.make_async_copy(volts_hbm, volts, fetched.at[0]),
        pltpu.make_async_copy(taps_hbm, taps, fetched.at[1]),
        pltpu.make_async_copy(table_hbm, table, fetched.at[2]),
    ]
    for copy in fetch:
        copy.start()
    fetch[0].wait()
    fetch[1].wait()

    def filter_lanes(mb, _):
        base = pl.multiple_of(mb * 128, 128)
        weights = [jnp.broadcast_to(taps[t : t + 1, pl.ds(base, 128)], (inp, 128)) for t in range(ntaps)]

        def block(s):
            at = pl.multiple_of(s * frame + base, 128)
            return volts[:, pl.ds(at, 128)].astype(jnp.float32)

        held = [block(s) for s in range(ntaps - 1)]
        for s in range(spectra):
            held.append(block(s + ntaps - 1))
            total = weights[0] * held[0]
            for t in range(1, ntaps):
                total = total + weights[t] * held[t]
            frames.at[mb][pl.ds(s * inp, inp), :] = total
            held = held[1:]
        return 0

    lax.fori_loop(0, frame // 128, filter_lanes, 0)
    for mb in range(frame // 128):
        for i in range(inp):
            framesb[i * spectra : (i + 1) * spectra, mb * 128 : (mb + 1) * 128] = (
                frames.at[mb][pl.ds(i, spectra, stride=inp), :].astype(jnp.bfloat16)
            )

    fetch[2].wait()
    low = lax.broadcasted_iota(jnp.int32, (half, 128), 1) < spectra
    share = pairs // parts

    def channelize(part):
        rows = table[2 * half * part : 2 * half * (part + 1), :]
        product[...] = lax.dot_general(rows, framesb[...], NT, preferred_element_type=jnp.float32)
        for p in range(inp // 2):
            even = product[:half, 128 * p : 128 * (p + 1)]
            odd = product[half:, 128 * p : 128 * (p + 1)]
            chan_f[pl.ds(2 * p, half, stride=inp), :] = jnp.where(low, even, pltpu.roll(odd, spectra, 1))
            chan_f[pl.ds(2 * p + 1, half, stride=inp), :] = jnp.where(low, pltpu.roll(even, spectra, 1), odd)
        chan_send[:, share * part : share * (part + 1)] = (
            chan_f[...].reshape(m, share, inp, 128).astype(jnp.bfloat16)
        )

    def remote(src, dst, send_sem, recv_sem, peer):
        return pltpu.make_async_remote_copy(
            src_ref=src, dst_ref=dst, send_sem=send_sem, recv_sem=recv_sem,
            device_id=(groups, peer), device_id_type=pl.DeviceIdType.MESH,
        )

    def arrived(whole, kind, c):
        remote(whole, whole, sent.at[kind], got.at[kind, c], (1 - side) * m + place).wait_recv()

    def departed(whole, kind):
        remote(whole, whole, sent.at[kind], got.at[kind, 0], (1 - side) * m + place).wait_send()

    def full_chan(c, owner_side, q):
        at = pl.ds(c * step, step)
        return remote(
            chan_send.at[2 * q + owner_side, at], chan_recv.at[me, at],
            sent.at[0], got.at[0, c], owner_side * m + (1 - owner_side) * h + q,
        )

    def half_chan(c, q):
        at = pl.ds(c * step, step)
        return remote(
            chan_send.at[2 * q + 1 - side, at], chan_half.at[place, at],
            sent.at[0], got.at[1, c], side * (m + h) + q,
        )

    def full_vis(c, spot, source):
        at = pl.ds(c * step, step)
        return remote(
            vis_send.at[spot, at], vis_out.at[source, at],
            sent.at[2], got.at[2, c], side * m + spot,
        )

    def half_vis(c, spot, source):
        at = pl.ds(c * step, step)
        return remote(
            half_send.at[spot, at], packed_out.at[side, source, at],
            sent.at[3], got.at[3, c], side * m + spot,
        )

    def cross_vis(c, spot, source, column_side):
        at = pl.ds(c * step, step)
        return remote(
            cross_send.at[spot, at], packed_out.at[column_side, source, at],
            sent.at[4], got.at[4, c], (1 - side) * m + spot,
        )

    def loop(act):
        def body(p, _):
            act(lax.rem(place + p, m))
            return 0

        lax.fori_loop(0, m, body, 0)

    def send_chan(c):
        def body(p, _):
            q = lax.rem(spot_of + p, h)
            full_chan(c, 1 - side, q).start()

            @pl.when(jnp.logical_not(inner) | (q != spot_of))
            def _():
                full_chan(c, side, q).start()

            @pl.when(inner | (q != spot_of))
            def _():
                half_chan(c, q).start()

            return 0

        lax.fori_loop(0, h, body, 0)

    for part in range(parts):
        channelize(part)
        if part == 0:
            pl.semaphore_wait(barrier, n - 1)
        for c in range(part * chunks // parts, (part + 1) * chunks // parts):
            send_chan(c)

    @pl.when(inner)
    def _():
        chan_recv[me] = chan_send[2 * spot_of + side]

    @pl.when(jnp.logical_not(inner))
    def _():
        chan_half[place] = chan_send[2 * spot_of + 1 - side]

    scale = 1.0 / (spectra**0.5)
    ours = inputs // 2
    first = lax.broadcasted_iota(jnp.int32, (ours, 128), 1) < spectra

    def rows_of(value):
        return value.astype(jnp.float32).reshape(-1, 128)

    def product_of(left, right):
        return lax.dot_general(left, right, NT, preferred_element_type=jnp.float32) * scale

    def parities(value):
        return [
            jnp.where(first, value, 0.0).astype(jnp.bfloat16),
            jnp.where(first, 0.0, value).astype(jnp.bfloat16),
        ]

    @pl.when(inner)
    def _():
        for c in range(chunks):
            at = pl.ds(c * step, step)
            arrived(chan_recv.at[pl.ds(0, n - 1), at], 0, c)

            def gram(k, _):
                every = rows_of(chan_recv[:, k]).astype(jnp.bfloat16)
                own = parities(rows_of(chan_recv[pl.ds(side * m, m), k]))
                other = rows_of(chan_recv[pl.ds((1 - side) * m, m), k]).astype(jnp.bfloat16)
                cross = product_of(other, jnp.concatenate(own, axis=0))
                cross_send[:, k] = cross.reshape(m, inp, inputs).astype(jnp.bfloat16)
                for parity in range(2):
                    full = product_of(own[parity], every)
                    vis_send[:, k, parity] = full.reshape(m, inp, inputs).astype(jnp.bfloat16)
                return 0

            lax.fori_loop(c * step, (c + 1) * step, gram, 0)

            def scatter(spot):
                cross_vis(c, spot, spot_of, side).start()

                @pl.when(spot != place)
                def _():
                    full_vis(c, spot, spot_of).start()

            loop(scatter)

    @pl.when(jnp.logical_not(inner))
    def _():
        for c in range(chunks):
            at = pl.ds(c * step, step)
            arrived(chan_half.at[pl.ds(0, m - 1), at], 1, c)

            def gram(k, _):
                mine = rows_of(chan_half[:, k])
                within = product_of(mine.astype(jnp.bfloat16), jnp.concatenate(parities(mine), axis=0))
                half_send[:, k] = within.reshape(m, inp, inputs).astype(jnp.bfloat16)
                return 0

            lax.fori_loop(c * step, (c + 1) * step, gram, 0)

            def scatter(spot):
                @pl.when(spot != place)
                def _():
                    half_vis(c, spot, spot_of).start()

            loop(scatter)

    @pl.when(inner)
    def _():
        kept = pltpu.make_async_copy(vis_send.at[place], vis_out.at[spot_of], stored.at[0])
        kept.start()
        for c in range(chunks):
            at = pl.ds(c * step, step)
            arrived(vis_out.at[pl.ds(0, h - 1), at], 2, c)
            arrived(packed_out.at[side, pl.ds(0, h), at], 3, c)
        departed(vis_send.at[pl.ds(0, m - 1)], 2)
        departed(cross_send.at[pl.ds(0, m)], 4)
        kept.wait()

    @pl.when(jnp.logical_not(inner))
    def _():
        kept = pltpu.make_async_copy(half_send.at[place], packed_out.at[side, spot_of], stored.at[0])
        kept.start()
        for c in range(chunks):
            at = pl.ds(c * step, step)
            arrived(vis_out.at[pl.ds(0, h), at], 2, c)
            arrived(packed_out.at[side, pl.ds(0, h - 1), at], 3, c)
        departed(half_send.at[pl.ds(0, m - 1)], 3)
        kept.wait()

    for c in range(chunks):
        arrived(packed_out.at[1 - side, pl.ds(0, h), pl.ds(c * step, step)], 4, c)
    departed(chan_recv.at[pl.ds(0, 3 * h - 1)], 0)


def smooth_all(vis_in, packed, kernel, out_hbm, vis, rows_f, planes, window, out, stored):
    h, pairs, _, inp, inputs = vis_in.shape
    side = lax.div(lax.axis_index("freq"), 2 * h)
    channels = out.shape[0]
    ours = inputs // 2
    count = kernel.shape[1]
    reach = (count - 1) // 2
    window[...] = jnp.zeros_like(window)
    window[0:1, 0:count] = kernel[...].astype(jnp.bfloat16).astype(jnp.float32)
    spread = jnp.broadcast_to(window[0:1, :], (128, 256))
    band = pltpu.roll(spread, 64 - reach, 1, stride=1, stride_axis=0).astype(jnp.bfloat16)
    lower = lax.broadcasted_iota(jnp.int32, (pairs, inp, inputs), 2) < ours

    def unpack(spot, _):
        left = packed[0, spot].astype(jnp.float32)
        right = packed[1, spot].astype(jnp.float32)
        even = jnp.where(lower, left, pltpu.roll(right, ours, 2))
        odd = jnp.where(lower, pltpu.roll(left, ours, 2), right)
        vis[spot, 1 - side, :, 0] = even.astype(jnp.bfloat16)
        vis[spot, 1 - side, :, 1] = odd.astype(jnp.bfloat16)
        vis[spot, side] = vis_in[spot]
        return 0

    lax.fori_loop(0, h, unpack, 0)

    planes[0:64, :] = jnp.zeros((64, inp * 128), jnp.bfloat16)
    planes[64 + channels :, :] = jnp.zeros((64, inp * 128), jnp.bfloat16)

    def smooth(j, _):
        lanes = pl.ds(pl.multiple_of(j * 128, 128), 128)
        rows_f[...] = vis[:, :, :, :, :, lanes].astype(jnp.float32).reshape(channels * inp, 128)
        for i in range(inp):
            planes[64 : 64 + channels, i * 128 : (i + 1) * 128] = (
                rows_f[pl.ds(i, channels, stride=inp), :].astype(jnp.bfloat16)
            )
        for r in range(channels // 128):
            done = jnp.dot(band, planes[r * 128 : r * 128 + 256, :], preferred_element_type=jnp.float32)
            for i in range(inp):
                rows_f[pl.ds(r * 128 * inp + i, 128, stride=inp), :] = done[:, i * 128 : (i + 1) * 128]
            rows = rows_f[r * 128 * inp : (r + 1) * 128 * inp, :]
            out[r * 128 : (r + 1) * 128, :, lanes] = rows.reshape(128, inp, 128).astype(jnp.bfloat16)
            pltpu.make_async_copy(
                out.at[r * 128 : (r + 1) * 128, :, lanes],
                out_hbm.at[r * 128 : (r + 1) * 128, :, lanes],
                stored.at[0],
            ).start()
        return 0

    lax.fori_loop(0, inputs // 128, smooth, 0)
    pltpu.make_async_copy(out, out_hbm, stored.at[0]).wait()


def shards(volts, filter_taps, kernel):
    inp, samples = volts.shape
    ntaps, frame = filter_taps.shape
    channels = frame // 2
    spectra = samples // frame - ntaps + 1
    n = lax.axis_size("freq")
    owners = n // 2
    pairs = channels // owners // 2
    inputs = n * inp
    chunks = min(CHUNKS, pairs)
    parts = min(PARTS, chunks)
    table = jnp.asarray(make_table(frame, channels, owners, parts))
    vmem = pl.BlockSpec(memory_space=pltpu.VMEM)
    hbm = pl.BlockSpec(memory_space=pl.ANY)
    far = pl.BlockSpec(memory_space=pltpu.HBM)
    bf16, f32 = jnp.bfloat16, jnp.float32
    half = owners // 2
    vis, packed = pl.pallas_call(
        functools.partial(correlate, n, chunks, parts),
        out_shape=[
            jax.ShapeDtypeStruct((half, pairs, 2, inp, inputs), bf16),
            jax.ShapeDtypeStruct((2, half, pairs, inp, inputs), bf16),
        ],
        in_specs=[far, far, far],
        out_specs=[hbm, hbm],
        scratch_shapes=[
            pltpu.VMEM(volts.shape, bf16),
            pltpu.VMEM(filter_taps.shape, f32),
            pltpu.VMEM(table.shape, bf16),
            pltpu.VMEM((frame // 128, inp * spectra, 128), f32),
            pltpu.VMEM((inp * spectra, frame), bf16),
            pltpu.VMEM((channels // parts, inp * spectra), f32),
            pltpu.VMEM((channels // parts // 2 * inp, 128), f32),
            pltpu.VMEM((n // 2, pairs, inp, 128), bf16),
            pltpu.VMEM((n, pairs, inp, 128), bf16),
            pltpu.VMEM((n // 2, pairs, inp, 128), bf16),
            pltpu.VMEM((n // 2, pairs, 2, inp, inputs), bf16),
            pltpu.VMEM((n // 2, pairs, inp, inputs), bf16),
            pltpu.VMEM((n // 2, pairs, inp, inputs), bf16),
            pltpu.SemaphoreType.DMA((5,)),
            pltpu.SemaphoreType.DMA((5, chunks)),
            pltpu.SemaphoreType.DMA((3,)),
            pltpu.SemaphoreType.DMA((1,)),
        ],
        compiler_params=pltpu.CompilerParams(
            collective_id=0, has_side_effects=True, vmem_limit_bytes=52 << 20
        ),
        name="correlate",
    )(*[pltpu.with_memory_space_constraint(x, pltpu.HBM) for x in (volts, filter_taps, table)])
    return pl.pallas_call(
        smooth_all,
        out_shape=jax.ShapeDtypeStruct((channels, inp, inputs), bf16),
        in_specs=[vmem, vmem, vmem],
        out_specs=hbm,
        scratch_shapes=[
            pltpu.VMEM((half, 2, pairs, 2, inp, inputs), bf16),
            pltpu.VMEM((channels * inp, 128), f32),
            pltpu.VMEM((channels + 128, inp * 128), bf16),
            pltpu.VMEM((8, 256), f32),
            pltpu.VMEM((channels, inp, inputs), bf16),
            pltpu.SemaphoreType.DMA((1,)),
        ],
        compiler_params=pltpu.CompilerParams(vmem_limit_bytes=24 << 20),
        name="smooth",
    )(vis, packed, kernel.reshape(1, -1))


def solution(mesh):
    return jax.shard_map(
        shards,
        mesh=mesh,
        in_specs=(P(("groups", "freq"), None), P(), P()),
        out_specs=P(None, ("groups", "freq"), None),
        check_vma=False,
    )
```

```python
import functools

import jax
import jax.numpy as jnp
import ml_dtypes
import numpy as np
from jax import lax
from jax.experimental import pallas as pl
from jax.experimental.pallas import tpu as pltpu
from jax.sharding import PartitionSpec as P

CHUNKS = 8
PARTS = 2
NT = (((1,), (1,)), ((), ()))


def make_table(frame, channels, owners, parts):
    order = np.arange(channels).reshape(owners, parts, channels // owners // parts // 2, 2)
    order = order.transpose(1, 3, 0, 2).reshape(-1)
    rows = np.arange(frame)
    phase = (2 * rows[None, :] + 1 + channels) * (2 * order[:, None] + 1) % (8 * channels)
    angle = phase.astype(np.float32) * np.float32(np.pi / (4.0 * channels))
    scale = np.float32(1.0) / np.sqrt(np.float32(channels))
    return (np.cos(angle) * scale).astype(ml_dtypes.bfloat16)


def correlate(
    n, chunks, parts, volts_hbm, taps_hbm, table_hbm, vis_out, packed_out,
    volts, taps, table,
    frames, framesb, product, chan_f, chan_send, chan_recv, chan_half,
    vis_send, half_send, cross_send,
    sent, got, fetched, stored, ready,
):
    groups = lax.axis_index("groups")
    me = lax.axis_index("freq")
    m = n // 2
    h = m // 2
    side = lax.div(me, m)
    place = lax.rem(me, m)
    spot_of = lax.rem(place, h)
    inner = lax.div(place, h) != side
    ntaps, frame = taps.shape
    channels = table.shape[0]
    inp, samples = volts.shape
    spectra = samples // frame - ntaps + 1
    pairs = channels // m // 2
    step = pairs // chunks
    inputs = n * inp
    half = channels // 2 // parts

    barrier = pltpu.get_barrier_semaphore()

    fetch = [
        pltpu.make_async_copy(volts_hbm, volts, fetched.at[0]),
        pltpu.make_async_copy(taps_hbm, taps, fetched.at[1]),
        pltpu.make_async_copy(table_hbm, table, fetched.at[2]),
    ]
    for copy in fetch:
        copy.start()
    def greet(peer, _):
        @pl.when((peer != me) & (inner | is_outer_mate(peer)))
        def _():
            pl.semaphore_signal(
                barrier, inc=1, device_id=(groups, peer), device_id_type=pl.DeviceIdType.MESH
            )

        return 0

    def is_outer_mate(peer):
        on = lax.div(peer, m)
        return (on == side) & (lax.div(lax.rem(peer, m), h) == on)

    lax.fori_loop(0, n, greet, 0)

    fetch[0].wait()
    fetch[1].wait()

    def filter_lanes(mb, _):
        base = pl.multiple_of(mb * 128, 128)
        weights = [jnp.broadcast_to(taps[t : t + 1, pl.ds(base, 128)], (inp, 128)) for t in range(ntaps)]

        def block(s):
            at = pl.multiple_of(s * frame + base, 128)
            return volts[:, pl.ds(at, 128)].astype(jnp.float32)

        held = [block(s) for s in range(ntaps - 1)]
        for s in range(spectra):
            held.append(block(s + ntaps - 1))
            total = weights[0] * held[0]
            for t in range(1, ntaps):
                total = total + weights[t] * held[t]
            frames.at[mb][pl.ds(s * inp, inp), :] = total
            held = held[1:]
        return 0

    lax.fori_loop(0, frame // 128, filter_lanes, 0, unroll=2)
    for mb in range(frame // 128):
        for i in range(inp):
            framesb[i * spectra : (i + 1) * spectra, mb * 128 : (mb + 1) * 128] = (
                frames.at[mb][pl.ds(i, spectra, stride=inp), :].astype(jnp.bfloat16)
            )

    fetch[2].wait()
    low = lax.broadcasted_iota(jnp.int32, (half, 128), 1) < spectra
    share = pairs // parts

    def channelize(part):
        rows = table[2 * half * part : 2 * half * (part + 1), :]
        product[...] = lax.dot_general(rows, framesb[...], NT, preferred_element_type=jnp.float32)
        for p in range(inp // 2):
            even = product[:half, 128 * p : 128 * (p + 1)]
            odd = product[half:, 128 * p : 128 * (p + 1)]
            chan_f[pl.ds(2 * p, half, stride=inp), :] = jnp.where(low, even, pltpu.roll(odd, spectra, 1))
            chan_f[pl.ds(2 * p + 1, half, stride=inp), :] = jnp.where(low, pltpu.roll(even, spectra, 1), odd)
        chan_send[:, share * part : share * (part + 1)] = (
            chan_f[...].reshape(m, share, inp, 128).astype(jnp.bfloat16)
        )

    def remote(src, dst, send_sem, recv_sem, peer):
        return pltpu.make_async_remote_copy(
            src_ref=src, dst_ref=dst, send_sem=send_sem, recv_sem=recv_sem,
            device_id=(groups, peer), device_id_type=pl.DeviceIdType.MESH,
        )

    def arrived(whole, kind, c):
        remote(whole, whole, sent.at[kind], got.at[kind, c], (1 - side) * m + place).wait_recv()

    def departed(whole, kind):
        remote(whole, whole, sent.at[kind], got.at[kind, 0], (1 - side) * m + place).wait_send()

    def full_chan(c, owner_side, q):
        at = pl.ds(c * step, step)
        return remote(
            chan_send.at[2 * q + owner_side, at], chan_recv.at[me, at],
            sent.at[0], got.at[0, c], owner_side * m + (1 - owner_side) * h + q,
        )

    def half_chan(c, q):
        at = pl.ds(c * step, step)
        return remote(
            chan_send.at[2 * q + 1 - side, at], chan_half.at[place, at],
            sent.at[0], got.at[1, c], side * (m + h) + q,
        )

    def full_vis(c, spot, source):
        at = pl.ds(c * step, step)
        return remote(
            vis_send.at[spot, at], vis_out.at[source, at],
            sent.at[2], got.at[2, c], side * m + spot,
        )

    def half_vis(c, spot, source):
        at = pl.ds(c * step, step)
        return remote(
            half_send.at[spot, at], packed_out.at[side, source, at],
            sent.at[3], got.at[3, c], side * m + spot,
        )

    def cross_vis(c, spot, source, column_side):
        at = pl.ds(c * step, step)
        return remote(
            cross_send.at[spot, at], packed_out.at[column_side, source, at],
            sent.at[4], got.at[4, c], (1 - side) * m + spot,
        )

    def loop(act):
        def body(p, _):
            act(lax.rem(place + p, m))
            return 0

        lax.fori_loop(0, m, body, 0)

    def send_other(c):
        def body(p, _):
            full_chan(c, 1 - side, lax.rem(spot_of + p, h)).start()
            return 0

        lax.fori_loop(0, h, body, 0)

    def send_own(c):
        def body(p, _):
            q = lax.rem(spot_of + p, h)

            @pl.when(jnp.logical_not(inner) | (q != spot_of))
            def _():
                full_chan(c, side, q).start()

            return 0

        lax.fori_loop(0, h, body, 0)

    def send_half(c):
        def body(p, _):
            q = lax.rem(spot_of + p, h)

            @pl.when(inner | (q != spot_of))
            def _():
                half_chan(c, q).start()

            return 0

        lax.fori_loop(0, h, body, 0)

    def enter():
        @pl.when(inner)
        def _():
            pl.semaphore_wait(barrier, m - 1)

        @pl.when(jnp.logical_not(inner))
        def _():
            pl.semaphore_wait(barrier, m + h - 1)

            def tell(q, _):
                for on in range(2):
                    pl.semaphore_signal(
                        ready.at[lax.rem(on + side, 2)], inc=1, device_id=(groups, on * m + (1 - on) * h + q),
                        device_id_type=pl.DeviceIdType.MESH,
                    )
                return 0

            lax.fori_loop(0, h, tell, 0)

    for part in range(parts):
        channelize(part)
        if part == 0:
            enter()
        for c in range(part * chunks // parts, (part + 1) * chunks // parts):
            send_other(c)
        for c in range(part * chunks // parts, (part + 1) * chunks // parts):
            send_own(c)

    @pl.when(inner)
    def _():
        pl.semaphore_wait(ready.at[0], h)

    for c in range(chunks):
        send_half(c)

    @pl.when(inner)
    def _():
        chan_recv[me] = chan_send[2 * spot_of + side]

    @pl.when(jnp.logical_not(inner))
    def _():
        chan_half[place] = chan_send[2 * spot_of + 1 - side]

    scale = 1.0 / (spectra**0.5)
    ours = inputs // 2
    first = lax.broadcasted_iota(jnp.int32, (ours, 128), 1) < spectra

    def rows_of(value):
        return value.astype(jnp.float32).reshape(-1, 128)

    def product_of(left, right):
        return lax.dot_general(left, right, NT, preferred_element_type=jnp.float32) * scale

    def parities(value):
        return [
            jnp.where(first, value, 0.0).astype(jnp.bfloat16),
            jnp.where(first, 0.0, value).astype(jnp.bfloat16),
        ]

    @pl.when(inner)
    def _():
        for c in range(chunks):
            at = pl.ds(c * step, step)
            arrived(chan_recv.at[pl.ds(0, n - 1), at], 0, c)

            def gram(k, _):
                every = rows_of(chan_recv[:, k]).astype(jnp.bfloat16)
                own = parities(rows_of(chan_recv[pl.ds(side * m, m), k]))
                other = rows_of(chan_recv[pl.ds((1 - side) * m, m), k]).astype(jnp.bfloat16)
                cross = product_of(other, jnp.concatenate(own, axis=0))
                cross_send[:, k] = cross.reshape(m, inp, inputs).astype(jnp.bfloat16)
                for parity in range(2):
                    full = product_of(own[parity], every)
                    vis_send[:, k, parity] = full.reshape(m, inp, inputs).astype(jnp.bfloat16)
                return 0

            lax.fori_loop(c * step, (c + 1) * step, gram, 0)
            if c == 0:
                pl.semaphore_wait(ready.at[1], h)

            def scatter(spot):
                cross_vis(c, spot, spot_of, side).start()

                @pl.when(spot != place)
                def _():
                    full_vis(c, spot, spot_of).start()

            loop(scatter)

    @pl.when(jnp.logical_not(inner))
    def _():
        for c in range(chunks):
            at = pl.ds(c * step, step)
            arrived(chan_half.at[pl.ds(0, m - 1), at], 1, c)

            def gram(k, _):
                mine = rows_of(chan_half[:, k])
                within = product_of(mine.astype(jnp.bfloat16), jnp.concatenate(parities(mine), axis=0))
                half_send[:, k] = within.reshape(m, inp, inputs).astype(jnp.bfloat16)
                return 0

            lax.fori_loop(c * step, (c + 1) * step, gram, 0)

            def scatter(spot):
                @pl.when(spot != place)
                def _():
                    half_vis(c, spot, spot_of).start()

            loop(scatter)

    @pl.when(inner)
    def _():
        kept = pltpu.make_async_copy(vis_send.at[place], vis_out.at[spot_of], stored.at[0])
        kept.start()
        for c in range(chunks):
            at = pl.ds(c * step, step)
            arrived(vis_out.at[pl.ds(0, h - 1), at], 2, c)
            arrived(packed_out.at[side, pl.ds(0, h), at], 3, c)
        departed(vis_send.at[pl.ds(0, m - 1)], 2)
        departed(cross_send.at[pl.ds(0, m)], 4)
        kept.wait()

    @pl.when(jnp.logical_not(inner))
    def _():
        kept = pltpu.make_async_copy(half_send.at[place], packed_out.at[side, spot_of], stored.at[0])
        kept.start()
        for c in range(chunks):
            at = pl.ds(c * step, step)
            arrived(vis_out.at[pl.ds(0, h), at], 2, c)
            arrived(packed_out.at[side, pl.ds(0, h - 1), at], 3, c)
        departed(half_send.at[pl.ds(0, m - 1)], 3)
        kept.wait()

    for c in range(chunks):
        arrived(packed_out.at[1 - side, pl.ds(0, h), pl.ds(c * step, step)], 4, c)
    departed(chan_recv.at[pl.ds(0, 3 * h - 1)], 0)


def smooth_all(vis_in, packed, kernel, out_hbm, rows_f, planes, window, out, stored):
    h, pairs, _, inp, inputs = vis_in.shape
    side = lax.div(lax.axis_index("freq"), 2 * h)
    channels = out.shape[0]
    ours = inputs // 2
    count = kernel.shape[1]
    reach = (count - 1) // 2
    window[...] = jnp.zeros_like(window)
    window[0:1, 0:count] = kernel[...].astype(jnp.bfloat16).astype(jnp.float32)
    spread = jnp.broadcast_to(window[0:1, :], (128, 256))
    band = pltpu.roll(spread, 64 - reach, 1, stride=1, stride_axis=0).astype(jnp.bfloat16)
    lower = lax.broadcasted_iota(jnp.int32, (pairs, inp, inputs), 2) < ours
    size = pairs * 2 * inp

    def unpack(spot, _):
        left = packed[0, spot].astype(jnp.float32)
        right = packed[1, spot].astype(jnp.float32)
        even = jnp.where(lower, left, pltpu.roll(right, ours, 2))
        odd = jnp.where(lower, pltpu.roll(left, ours, 2), right)
        theirs = jnp.stack([even, odd], axis=1).reshape(size, inputs)
        mine = vis_in[spot].astype(jnp.float32).reshape(size, inputs)
        for j in range(inputs // 128):
            lanes = slice(j * 128, (j + 1) * 128)
            rows_f[j, pl.ds((2 * spot + side) * size, size), :] = mine[:, lanes]
            rows_f[j, pl.ds((2 * spot + 1 - side) * size, size), :] = theirs[:, lanes]
        return 0

    lax.fori_loop(0, h, unpack, 0)

    planes[0:64, :] = jnp.zeros((64, inp * 128), jnp.bfloat16)
    planes[64 + channels :, :] = jnp.zeros((64, inp * 128), jnp.bfloat16)

    def smooth(j, _):
        lanes = pl.ds(pl.multiple_of(j * 128, 128), 128)
        held = rows_f.at[j]
        for i in range(inp):
            planes[64 : 64 + channels, i * 128 : (i + 1) * 128] = (
                held[pl.ds(i, channels, stride=inp), :].astype(jnp.bfloat16)
            )
        for r in range(channels // 128):
            done = jnp.dot(band, planes[r * 128 : r * 128 + 256, :], preferred_element_type=jnp.float32)
            for i in range(inp):
                held[pl.ds(r * 128 * inp + i, 128, stride=inp), :] = done[:, i * 128 : (i + 1) * 128]
            rows = held[r * 128 * inp : (r + 1) * 128 * inp, :]
            out[r * 128 : (r + 1) * 128, :, lanes] = rows.reshape(128, inp, 128).astype(jnp.bfloat16)
            pltpu.make_async_copy(
                out.at[r * 128 : (r + 1) * 128, :, lanes],
                out_hbm.at[r * 128 : (r + 1) * 128, :, lanes],
                stored.at[0],
            ).start()
        return 0

    lax.fori_loop(0, inputs // 128, smooth, 0)
    pltpu.make_async_copy(out, out_hbm, stored.at[0]).wait()


def shards(volts, filter_taps, kernel):
    inp, samples = volts.shape
    ntaps, frame = filter_taps.shape
    channels = frame // 2
    spectra = samples // frame - ntaps + 1
    n = lax.axis_size("freq")
    owners = n // 2
    pairs = channels // owners // 2
    inputs = n * inp
    chunks = min(CHUNKS, pairs)
    parts = min(PARTS, chunks)
    table = jnp.asarray(make_table(frame, channels, owners, parts))
    vmem = pl.BlockSpec(memory_space=pltpu.VMEM)
    hbm = pl.BlockSpec(memory_space=pl.ANY)
    far = pl.BlockSpec(memory_space=pltpu.HBM)
    bf16, f32 = jnp.bfloat16, jnp.float32
    half = owners // 2
    vis, packed = pl.pallas_call(
        functools.partial(correlate, n, chunks, parts),
        out_shape=[
            jax.ShapeDtypeStruct((half, pairs, 2, inp, inputs), bf16),
            jax.ShapeDtypeStruct((2, half, pairs, inp, inputs), bf16),
        ],
        in_specs=[far, far, far],
        out_specs=[hbm, hbm],
        scratch_shapes=[
            pltpu.VMEM(volts.shape, bf16),
            pltpu.VMEM(filter_taps.shape, f32),
            pltpu.VMEM(table.shape, bf16),
            pltpu.VMEM((frame // 128, inp * spectra, 128), f32),
            pltpu.VMEM((inp * spectra, frame), bf16),
            pltpu.VMEM((channels // parts, inp * spectra), f32),
            pltpu.VMEM((channels // parts // 2 * inp, 128), f32),
            pltpu.VMEM((n // 2, pairs, inp, 128), bf16),
            pltpu.VMEM((n, pairs, inp, 128), bf16),
            pltpu.VMEM((n // 2, pairs, inp, 128), bf16),
            pltpu.VMEM((n // 2, pairs, 2, inp, inputs), bf16),
            pltpu.VMEM((n // 2, pairs, inp, inputs), bf16),
            pltpu.VMEM((n // 2, pairs, inp, inputs), bf16),
            pltpu.SemaphoreType.DMA((5,)),
            pltpu.SemaphoreType.DMA((5, chunks)),
            pltpu.SemaphoreType.DMA((3,)),
            pltpu.SemaphoreType.DMA((1,)),
            pltpu.SemaphoreType.REGULAR((2,)),
        ],
        compiler_params=pltpu.CompilerParams(
            collective_id=0, has_side_effects=True, vmem_limit_bytes=52 << 20
        ),
        name="correlate",
    )(*[pltpu.with_memory_space_constraint(x, pltpu.HBM) for x in (volts, filter_taps, table)])
    return pl.pallas_call(
        smooth_all,
        out_shape=jax.ShapeDtypeStruct((channels, inp, inputs), bf16),
        in_specs=[vmem, vmem, vmem],
        out_specs=hbm,
        scratch_shapes=[
            pltpu.VMEM((inputs // 128, channels * inp, 128), f32),
            pltpu.VMEM((channels + 128, inp * 128), bf16),
            pltpu.VMEM((8, 256), f32),
            pltpu.VMEM((channels, inp, inputs), bf16),
            pltpu.SemaphoreType.DMA((1,)),
        ],
        compiler_params=pltpu.CompilerParams(vmem_limit_bytes=48 << 20),
        name="smooth",
    )(vis, packed, kernel.reshape(1, -1))


def solution(mesh):
    return jax.shard_map(
        shards,
        mesh=mesh,
        in_specs=(P(("groups", "freq"), None), P(), P()),
        out_specs=P(None, ("groups", "freq"), None),
        check_vma=False,
    )
```

```python
import functools

import jax
import jax.numpy as jnp
import ml_dtypes
import numpy as np
from jax import lax
from jax.experimental import pallas as pl
from jax.experimental.pallas import tpu as pltpu
from jax.sharding import PartitionSpec as P

CHUNKS = 8
PARTS = 2
NT = (((1,), (1,)), ((), ()))


def make_table(frame, channels, owners, parts):
    order = np.arange(channels).reshape(owners, parts, channels // owners // parts // 2, 2)
    order = order.transpose(1, 3, 0, 2).reshape(-1)
    rows = np.arange(frame)
    phase = (2 * rows[None, :] + 1 + channels) * (2 * order[:, None] + 1) % (8 * channels)
    angle = phase.astype(np.float32) * np.float32(np.pi / (4.0 * channels))
    scale = np.float32(1.0) / np.sqrt(np.float32(channels))
    return (np.cos(angle) * scale).astype(ml_dtypes.bfloat16)


def correlate(
    n, chunks, parts, volts_hbm, taps_hbm, table_hbm, vis_out, packed_out,
    volts, taps, table,
    frames, framesb, product, chan_f, chan_send, chan_recv, chan_half,
    vis_send, half_send, cross_send,
    sent, got, fetched, stored, ready,
):
    groups = lax.axis_index("groups")
    me = lax.axis_index("freq")
    m = n // 2
    h = m // 2
    side = lax.div(me, m)
    place = lax.rem(me, m)
    spot_of = lax.rem(place, h)
    inner = lax.div(place, h) != side
    ntaps, frame = taps.shape
    channels = table.shape[0]
    inp, samples = volts.shape
    spectra = samples // frame - ntaps + 1
    pairs = channels // m // 2
    step = pairs // chunks
    inputs = n * inp
    half = channels // 2 // parts

    barrier = pltpu.get_barrier_semaphore()

    fetch = [
        pltpu.make_async_copy(volts_hbm, volts, fetched.at[0]),
        pltpu.make_async_copy(taps_hbm, taps, fetched.at[1]),
        pltpu.make_async_copy(table_hbm, table, fetched.at[2]),
    ]
    for copy in fetch:
        copy.start()
    def greet(peer, _):
        @pl.when((peer != me) & (inner | is_outer_mate(peer)))
        def _():
            pl.semaphore_signal(
                barrier, inc=1, device_id=(groups, peer), device_id_type=pl.DeviceIdType.MESH
            )

        return 0

    def is_outer_mate(peer):
        on = lax.div(peer, m)
        return (on == side) & (lax.div(lax.rem(peer, m), h) == on)

    lax.fori_loop(0, n, greet, 0)

    fetch[0].wait()
    fetch[1].wait()

    def filter_lanes(mb, _):
        base = pl.multiple_of(mb * 128, 128)
        weights = [jnp.broadcast_to(taps[t : t + 1, pl.ds(base, 128)], (inp, 128)) for t in range(ntaps)]

        def block(s):
            at = pl.multiple_of(s * frame + base, 128)
            return volts[:, pl.ds(at, 128)].astype(jnp.float32)

        held = [block(s) for s in range(ntaps - 1)]
        for s in range(spectra):
            held.append(block(s + ntaps - 1))
            total = weights[0] * held[0]
            for t in range(1, ntaps):
                total = total + weights[t] * held[t]
            frames.at[mb][pl.ds(s * inp, inp), :] = total
            held = held[1:]
        return 0

    lax.fori_loop(0, frame // 128, filter_lanes, 0, unroll=2)
    for mb in range(frame // 128):
        for i in range(inp):
            framesb[i * spectra : (i + 1) * spectra, mb * 128 : (mb + 1) * 128] = (
                frames.at[mb][pl.ds(i, spectra, stride=inp), :].astype(jnp.bfloat16)
            )

    fetch[2].wait()
    low = lax.broadcasted_iota(jnp.int32, (half, 128), 1) < spectra
    share = pairs // parts

    def channelize(part):
        rows = table[2 * half * part : 2 * half * (part + 1), :]
        product[...] = lax.dot_general(rows, framesb[...], NT, preferred_element_type=jnp.float32)
        for p in range(inp // 2):
            even = product[:half, 128 * p : 128 * (p + 1)]
            odd = product[half:, 128 * p : 128 * (p + 1)]
            chan_f[pl.ds(2 * p, half, stride=inp), :] = jnp.where(low, even, pltpu.roll(odd, spectra, 1))
            chan_f[pl.ds(2 * p + 1, half, stride=inp), :] = jnp.where(low, pltpu.roll(even, spectra, 1), odd)
        chan_send[:, share * part : share * (part + 1)] = (
            chan_f[...].reshape(m, share, inp, 128).astype(jnp.bfloat16)
        )

    def remote(src, dst, send_sem, recv_sem, peer):
        return pltpu.make_async_remote_copy(
            src_ref=src, dst_ref=dst, send_sem=send_sem, recv_sem=recv_sem,
            device_id=(groups, peer), device_id_type=pl.DeviceIdType.MESH,
        )

    def arrived(whole, kind, c):
        remote(whole, whole, sent.at[kind], got.at[kind, c], (1 - side) * m + place).wait_recv()

    def departed(whole, kind):
        remote(whole, whole, sent.at[kind], got.at[kind, 0], (1 - side) * m + place).wait_send()

    def full_chan(c, owner_side, q):
        at = pl.ds(c * step, step)
        return remote(
            chan_send.at[2 * q + owner_side, at], chan_recv.at[me, at],
            sent.at[0], got.at[0, c], owner_side * m + (1 - owner_side) * h + q,
        )

    def half_chan(c, q):
        at = pl.ds(c * step, step)
        return remote(
            chan_send.at[2 * q + 1 - side, at], chan_half.at[place, at],
            sent.at[0], got.at[1, c], side * (m + h) + q,
        )

    def full_vis(c, spot, source):
        at = pl.ds(c * step, step)
        return remote(
            vis_send.at[spot, at], vis_out.at[source, at],
            sent.at[2], got.at[2, c], side * m + spot,
        )

    def half_vis(c, spot, source):
        at = pl.ds(c * step, step)
        return remote(
            half_send.at[spot, at], packed_out.at[side, source, at],
            sent.at[3], got.at[3, c], side * m + spot,
        )

    def cross_vis(c, spot, source, column_side):
        at = pl.ds(c * step, step)
        return remote(
            cross_send.at[spot, at], packed_out.at[column_side, source, at],
            sent.at[4], got.at[4, c], (1 - side) * m + spot,
        )

    def loop(act):
        def body(p, _):
            act(lax.rem(place + p, m))
            return 0

        lax.fori_loop(0, m, body, 0)

    def send_other(c):
        def body(p, _):
            full_chan(c, 1 - side, lax.rem(spot_of + p, h)).start()
            return 0

        lax.fori_loop(0, h, body, 0)

    def send_own(c):
        def body(p, _):
            q = lax.rem(spot_of + p, h)

            @pl.when(jnp.logical_not(inner) | (q != spot_of))
            def _():
                full_chan(c, side, q).start()

            return 0

        lax.fori_loop(0, h, body, 0)

    def send_half(c):
        def body(p, _):
            q = lax.rem(spot_of + p, h)

            @pl.when(inner | (q != spot_of))
            def _():
                half_chan(c, q).start()

            return 0

        lax.fori_loop(0, h, body, 0)

    def enter():
        @pl.when(inner)
        def _():
            pl.semaphore_wait(barrier, m - 1)

        @pl.when(jnp.logical_not(inner))
        def _():
            pl.semaphore_wait(barrier, m + h - 1)

            def tell(q, _):
                for on in range(2):
                    pl.semaphore_signal(
                        ready.at[lax.rem(on + side, 2)], inc=1, device_id=(groups, on * m + (1 - on) * h + q),
                        device_id_type=pl.DeviceIdType.MESH,
                    )
                return 0

            lax.fori_loop(0, h, tell, 0)

    for part in range(parts):
        channelize(part)
        if part == 0:
            enter()
        for c in range(part * chunks // parts, (part + 1) * chunks // parts):
            send_other(c)
        for c in range(part * chunks // parts, (part + 1) * chunks // parts):
            send_own(c)

    @pl.when(inner)
    def _():
        pl.semaphore_wait(ready.at[0], h)

    for c in range(chunks):
        send_half(c)

    @pl.when(inner)
    def _():
        chan_recv[me] = chan_send[2 * spot_of + side]

    @pl.when(jnp.logical_not(inner))
    def _():
        chan_half[place] = chan_send[2 * spot_of + 1 - side]

    scale = 1.0 / (spectra**0.5)
    ours = inputs // 2
    first = lax.broadcasted_iota(jnp.int32, (ours, 128), 1) < spectra

    def rows_of(value):
        return value.astype(jnp.float32).reshape(-1, 128)

    def product_of(left, right):
        return lax.dot_general(left, right, NT, preferred_element_type=jnp.float32) * scale

    def parities(value):
        return [
            jnp.where(first, value, 0.0).astype(jnp.bfloat16),
            jnp.where(first, 0.0, value).astype(jnp.bfloat16),
        ]

    @pl.when(inner)
    def _():
        for c in range(chunks):
            at = pl.ds(c * step, step)
            arrived(chan_recv.at[pl.ds(0, n - 1), at], 0, c)

            def gram(k, _):
                every = rows_of(chan_recv[:, k]).astype(jnp.bfloat16)
                own = parities(rows_of(chan_recv[pl.ds(side * m, m), k]))
                other = rows_of(chan_recv[pl.ds((1 - side) * m, m), k]).astype(jnp.bfloat16)
                cross = product_of(other, jnp.concatenate(own, axis=0))
                cross_send[:, k] = cross.reshape(m, inp, inputs).astype(jnp.bfloat16)
                for parity in range(2):
                    full = product_of(own[parity], every)
                    vis_send[:, k, parity] = full.reshape(m, inp, inputs).astype(jnp.bfloat16)
                return 0

            lax.fori_loop(c * step, (c + 1) * step, gram, 0)
            if c == 0:
                pl.semaphore_wait(ready.at[1], h)

            def scatter(spot):
                cross_vis(c, spot, spot_of, side).start()

                @pl.when(spot != place)
                def _():
                    full_vis(c, spot, spot_of).start()

            loop(scatter)

    @pl.when(jnp.logical_not(inner))
    def _():
        for c in range(chunks):
            at = pl.ds(c * step, step)
            arrived(chan_half.at[pl.ds(0, m - 1), at], 1, c)

            def gram(k, _):
                mine = rows_of(chan_half[:, k])
                within = product_of(mine.astype(jnp.bfloat16), jnp.concatenate(parities(mine), axis=0))
                half_send[:, k] = within.reshape(m, inp, inputs).astype(jnp.bfloat16)
                return 0

            lax.fori_loop(c * step, (c + 1) * step, gram, 0)

            def scatter(spot):
                @pl.when(spot != place)
                def _():
                    half_vis(c, spot, spot_of).start()

            loop(scatter)

    @pl.when(inner)
    def _():
        kept = pltpu.make_async_copy(vis_send.at[place], vis_out.at[spot_of], stored.at[0])
        kept.start()
        for c in range(chunks):
            at = pl.ds(c * step, step)
            arrived(vis_out.at[pl.ds(0, h - 1), at], 2, c)
            arrived(packed_out.at[side, pl.ds(0, h), at], 3, c)
        departed(vis_send.at[pl.ds(0, m - 1)], 2)
        departed(cross_send.at[pl.ds(0, m)], 4)
        kept.wait()

    @pl.when(jnp.logical_not(inner))
    def _():
        kept = pltpu.make_async_copy(half_send.at[place], packed_out.at[side, spot_of], stored.at[0])
        kept.start()
        for c in range(chunks):
            at = pl.ds(c * step, step)
            arrived(vis_out.at[pl.ds(0, h), at], 2, c)
            arrived(packed_out.at[side, pl.ds(0, h - 1), at], 3, c)
        departed(half_send.at[pl.ds(0, m - 1)], 3)
        kept.wait()

    for c in range(chunks):
        arrived(packed_out.at[1 - side, pl.ds(0, h), pl.ds(c * step, step)], 4, c)
    departed(chan_recv.at[pl.ds(0, 3 * h - 1)], 0)


def smooth_all(vis_in, packed, kernel, out_hbm, rows_f, planes, window, results, out, stored):
    h, pairs, _, inp, inputs = vis_in.shape
    side = lax.div(lax.axis_index("freq"), 2 * h)
    channels = out.shape[0]
    ours = inputs // 2
    count = kernel.shape[1]
    reach = (count - 1) // 2
    window[...] = jnp.zeros_like(window)
    window[0:1, 0:count] = kernel[...].astype(jnp.bfloat16).astype(jnp.float32)
    spread = jnp.broadcast_to(window[0:1, :], (128, 256))
    band = pltpu.roll(spread, 64 - reach, 1, stride=1, stride_axis=0).astype(jnp.bfloat16)
    lower = lax.broadcasted_iota(jnp.int32, (pairs, inp, inputs), 2) < ours
    size = pairs * 2 * inp

    def unpack(spot, _):
        left = packed[0, spot].astype(jnp.float32)
        right = packed[1, spot].astype(jnp.float32)
        crossed = pltpu.roll(jnp.where(lower, right, left), ours, 2)
        even = jnp.where(lower, left, crossed)
        odd = jnp.where(lower, crossed, right)
        theirs = jnp.stack([even, odd], axis=1).reshape(size, inputs)
        mine = vis_in[spot].astype(jnp.float32).reshape(size, inputs)
        for j in range(inputs // 128):
            lanes = slice(j * 128, (j + 1) * 128)
            rows_f[j, pl.ds((2 * spot + side) * size, size), :] = mine[:, lanes]
            rows_f[j, pl.ds((2 * spot + 1 - side) * size, size), :] = theirs[:, lanes]
        return 0

    lax.fori_loop(0, h, unpack, 0, unroll=4)

    planes[0:64, :] = jnp.zeros((64, inp * 128), jnp.bfloat16)
    planes[64 + channels :, :] = jnp.zeros((64, inp * 128), jnp.bfloat16)

    def smooth(j, _):
        lanes = pl.ds(pl.multiple_of(j * 128, 128), 128)
        held = rows_f.at[j]
        for i in range(inp):
            planes[64 : 64 + channels, i * 128 : (i + 1) * 128] = (
                held[pl.ds(i, channels, stride=inp), :].astype(jnp.bfloat16)
            )
        for r in range(channels // 128):
            done = jnp.dot(band, planes[r * 128 : r * 128 + 256, :], preferred_element_type=jnp.float32)
            for i in range(inp):
                results[r % 2, pl.ds(i, 128, stride=inp), :] = done[:, i * 128 : (i + 1) * 128]
            rows = results[r % 2]
            out[r * 128 : (r + 1) * 128, :, lanes] = rows.reshape(128, inp, 128).astype(jnp.bfloat16)
            pltpu.make_async_copy(
                out.at[r * 128 : (r + 1) * 128, :, lanes],
                out_hbm.at[r * 128 : (r + 1) * 128, :, lanes],
                stored.at[0],
            ).start()
        return 0

    lax.fori_loop(0, inputs // 128, smooth, 0)
    pltpu.make_async_copy(out, out_hbm, stored.at[0]).wait()


def shards(volts, filter_taps, kernel):
    inp, samples = volts.shape
    ntaps, frame = filter_taps.shape
    channels = frame // 2
    spectra = samples // frame - ntaps + 1
    n = lax.axis_size("freq")
    owners = n // 2
    pairs = channels // owners // 2
    inputs = n * inp
    chunks = min(CHUNKS, pairs)
    parts = min(PARTS, chunks)
    table = jnp.asarray(make_table(frame, channels, owners, parts))
    vmem = pl.BlockSpec(memory_space=pltpu.VMEM)
    hbm = pl.BlockSpec(memory_space=pl.ANY)
    far = pl.BlockSpec(memory_space=pltpu.HBM)
    bf16, f32 = jnp.bfloat16, jnp.float32
    half = owners // 2
    vis, packed = pl.pallas_call(
        functools.partial(correlate, n, chunks, parts),
        out_shape=[
            jax.ShapeDtypeStruct((half, pairs, 2, inp, inputs), bf16),
            jax.ShapeDtypeStruct((2, half, pairs, inp, inputs), bf16),
        ],
        in_specs=[far, far, far],
        out_specs=[hbm, hbm],
        scratch_shapes=[
            pltpu.VMEM(volts.shape, bf16),
            pltpu.VMEM(filter_taps.shape, f32),
            pltpu.VMEM(table.shape, bf16),
            pltpu.VMEM((frame // 128, inp * spectra, 128), f32),
            pltpu.VMEM((inp * spectra, frame), bf16),
            pltpu.VMEM((channels // parts, inp * spectra), f32),
            pltpu.VMEM((channels // parts // 2 * inp, 128), f32),
            pltpu.VMEM((n // 2, pairs, inp, 128), bf16),
            pltpu.VMEM((n, pairs, inp, 128), bf16),
            pltpu.VMEM((n // 2, pairs, inp, 128), bf16),
            pltpu.VMEM((n // 2, pairs, 2, inp, inputs), bf16),
            pltpu.VMEM((n // 2, pairs, inp, inputs), bf16),
            pltpu.VMEM((n // 2, pairs, inp, inputs), bf16),
            pltpu.SemaphoreType.DMA((5,)),
            pltpu.SemaphoreType.DMA((5, chunks)),
            pltpu.SemaphoreType.DMA((3,)),
            pltpu.SemaphoreType.DMA((1,)),
            pltpu.SemaphoreType.REGULAR((2,)),
        ],
        compiler_params=pltpu.CompilerParams(
            collective_id=0, has_side_effects=True, vmem_limit_bytes=52 << 20
        ),
        name="correlate",
    )(*[pltpu.with_memory_space_constraint(x, pltpu.HBM) for x in (volts, filter_taps, table)])
    return pl.pallas_call(
        smooth_all,
        out_shape=jax.ShapeDtypeStruct((channels, inp, inputs), bf16),
        in_specs=[vmem, vmem, vmem],
        out_specs=hbm,
        scratch_shapes=[
            pltpu.VMEM((inputs // 128, channels * inp, 128), f32),
            pltpu.VMEM((channels + 128, inp * 128), bf16),
            pltpu.VMEM((8, 256), f32),
            pltpu.VMEM((2, 128 * inp, 128), f32),
            pltpu.VMEM((channels, inp, inputs), bf16),
            pltpu.SemaphoreType.DMA((1,)),
        ],
        compiler_params=pltpu.CompilerParams(vmem_limit_bytes=48 << 20),
        name="smooth",
    )(vis, packed, kernel.reshape(1, -1))


def solution(mesh):
    return jax.shard_map(
        shards,
        mesh=mesh,
        in_specs=(P(("groups", "freq"), None), P(), P()),
        out_specs=P(None, ("groups", "freq"), None),
        check_vma=False,
    )
```
